256 devices in a mesh: row: 8 (over y_hi, x), col: 32 (over y_lo, z, core).
Axes of the slice: x: 4, y: 4 (y_hi: 2, y_lo: 2; y = y_hi * 2 + y_lo), z: 8, core: 2. Of those that a mesh axis runs over, the one named last changes fastest.
Arguments:
- sectors: int32 [96], replicated, may hold values from 0 to 7
- environment: bfloat16 [24576, 24576], P('col', 'row'), may hold values from -0.109375 to 0.109375
- wavefunction: bfloat16 [24576, 2048], P('row', 'col'), may hold values from -6 to 6
Outputs:
- applied: bfloat16 [24576, 2048], P('col', 'row')
The draws below stay inside these ranges and needn't reach their ends.
All inputs are finite; a program needn't handle non-finite values.
Results may differ from the reference program's by a relative error of at most 0.013.
Values may be sent and summed in bfloat16 or wider, within the bound.
A program may use at most 64 MiB of HBM per device.

```python
import jax
import jax.numpy as jnp
from jax import lax

BOND = 24576
BLOCK = 256
COLS = 2048
SECTORS = 8
BLOCKS = 96


def place_ends(result, rng, smallest, high):
    shape = result.shape
    place = [jax.random.randint(jax.random.fold_in(rng, axis), (), 0, shape[axis]) for axis in range(len(shape))]
    result = result.at[tuple(place)].set(smallest)
    longest = shape.index(max(shape))
    place[longest] = (place[longest] + 1) % shape[longest]
    return result.at[tuple(place)].set(high)


def block_scale(stream_key, dims, shards, smallest, top_value):
    gain, own = 1.0, jax.random.fold_in(stream_key, 6)
    for axis_at, parts in shards:
        heights = jnp.exp(jax.random.uniform(jax.random.fold_in(own, axis_at), (parts,), jnp.float32, smallest / len(shards), top_value / len(shards)))
        gain = gain * jnp.repeat(heights, dims[axis_at] // parts).reshape([-1 if axis == axis_at else 1 for axis in range(len(dims))])
    return gain


def gaussian(stream_key, extent, scale, limit, split=(), kind=jnp.bfloat16):
    array = jax.random.normal(stream_key, extent, jnp.float32) * scale
    if len(split) > 0:
        array = block_scale(stream_key, extent, split, -0.22, 0.18) * array
    return jnp.clip(array, min=-limit, max=limit).astype(kind)


def setup_inputs(seed: int = 0) -> dict:
    key_list = jax.random.split(jax.random.key(seed), 4)
    sectors = place_ends(jax.random.randint(key_list[0], (BLOCKS,), 0, SECTORS), jax.random.fold_in(key_list[0], 1), 0, SECTORS - 1).astype(jnp.int32)
    environment = gaussian(key_list[1], (BOND, BOND), (BOND // SECTORS) ** -0.5, 0.109375, ((0, 32), (1, 8)))
    wavefunction = gaussian(key_list[2], (BOND, COLS), 1.0, 6.0, ((0, 8), (1, 32)))
    return dict(sectors=sectors, environment=environment, wavefunction=wavefunction)


def reference(sectors, environment, wavefunction):
    panels = environment.reshape(BLOCKS, BLOCK, BOND)

    def block_rows(pair):
        row_panel, sector = pair
        allowed = jnp.repeat(sectors == sector, BLOCK)
        masked = jnp.where(allowed[None, :], row_panel, jnp.zeros_like(row_panel))
        return jnp.dot(masked, wavefunction, preferred_element_type=jnp.float32).astype(jnp.bfloat16)

    stacked = lax.map(block_rows, (panels, sectors))
    return stacked.reshape(BOND, COLS)
```

```python
import jax
import jax.numpy as jnp
from jax import lax
from jax.experimental import pallas as pl
from jax.experimental.pallas import tpu as pltpu
from jax.sharding import PartitionSpec as P

MESH = pl.DeviceIdType.MESH
BLOCK = 256
ITEM = 64
ROWS = 768
DEPTH = 3072
HALF = DEPTH // 2
TILE = 256
CHUNK = ROWS // 4

FULL = (0, ITEM, 0, DEPTH)
H0 = (0, ITEM, 0, HALF)
H1 = (0, ITEM, HALF, HALF)
H1LO = (0, ITEM // 2, HALF, HALF)
H1HI = (ITEM // 2, ITEM // 2, HALF, HALF)

ZP = [(0, 0, FULL), (1, 0, H1), (0, -1, FULL), (1, -1, H1), (0, -2, FULL), (1, -2, H1), (0, -3, H0), (1, -3, H1LO)]
ZM = [(0, 0, FULL), (1, 0, H1), (0, 1, FULL), (1, 1, H1), (0, 2, FULL), (1, 2, H1), (0, 3, H1), (1, 3, H1HI)]
YY = [(0, 0, H1), (0, 0, H0)] + [(0, s * d, H0) for d in (1, 2, 3) for s in (-1, 1)] + [(0, 4, H0)]
CC = [(0, 0, FULL), (1, 0, H1), (1, 0, H0)]
for _d in (1, 2, 3):
    CC += [(0, -_d, FULL), (0, _d, FULL), (1, -_d, H1), (1, _d, H1), (1, -_d, H0), (1, _d, H0)]
CC += [(0, 4, H0), (0, 4, H1), (1, 4, H1LO), (1, 4, H1HI), (1, 4, H0)]
LINKS = {"zp": ZP, "zm": ZM, "y": YY, "c": CC}


def kernel(sec_ref, env_ref, wave_ref, out_ref, a, g, cb, rb, red, fin,
           s_zp, r_zp, s_zm, r_zm, s_y, r_y, s_c, r_c, s_x, r_x, s_f, r_f, local):
    row, col = lax.axis_index("row"), lax.axis_index("col")
    yh, x = row // 4, row % 4
    y, z, c = col // 16, (col // 2) % 8, col % 2

    def device(dyh=0, dx=0, dy=0, dz=0, dc=0):
        return (
            (yh + dyh) % 2 * 4 + (x + dx) % 4,
            (y + dy) % 2 * 16 + (z + dz + 8) % 8 * 2 + (c + dc) % 2,
        )

    load_a = pltpu.make_async_copy(env_ref, a, local.at[0])
    load_a.start()
    own = pl.ds(pl.multiple_of(col * ITEM, ITEM), ITEM)
    load_b = pltpu.make_async_copy(wave_ref, g.at[own, :], local.at[1])
    load_b.start()

    barrier = pltpu.get_barrier_semaphore()
    greet = [device(dz=1), device(dz=-1), device(dy=1), device(dc=1)]
    greet += [device(dyh=h, dx=d) for h in (0, 1) for d in range(4) if (h, d) != (0, 0)]
    for peer in greet:
        pl.semaphore_signal(barrier, inc=1, device_id=peer, device_id_type=MESH)
    load_b.wait()
    pl.semaphore_wait(barrier, len(greet))

    sems = {"zp": (s_zp, r_zp), "zm": (s_zm, r_zm), "y": (s_y, r_y), "c": (s_c, r_c)}
    peers = {"zp": device(dz=1), "zm": device(dz=-1), "y": device(dy=1), "c": device(dc=1)}
    moves = {"zp": (0, -1, 0), "zm": (0, 1, 0), "y": (1, 0, 0), "c": (0, 0, 1)}

    def piece(line, d, part, parity):
        r0, nr, k0, nk = part
        j = (y + line) % 2 * 16 + (z + d + 8) % 8 * 2 + (c + parity) % 2
        return g.at[pl.ds(pl.multiple_of(j * ITEM + r0, 32), nr), pl.ds(k0, nk)]

    started = []

    def copy(link, ref, i):
        return pltpu.make_async_remote_copy(
            src_ref=ref, dst_ref=ref, send_sem=sems[link][0].at[i], recv_sem=sems[link][1].at[i],
            device_id=peers[link], device_id_type=MESH,
        )

    def send(link, line, d, part):
        i = LINKS[link].index((line, d, part))
        cp = copy(link, piece(line, d, part, 0), i)
        cp.start()
        started.append(cp)

    def recv(link, line, d, part):
        dl, dz, dc = moves[link]
        sd = d - dz
        sd = {-4: 4, 5: -3, -5: 3}.get(sd, sd)
        i = LINKS[link].index(((line + dl) % 2, sd, part))
        copy(link, piece(line, d, part, dc), i).wait_recv()

    def hop(link, line, d, part, onward):
        recv(link, line, d, part)
        for to, sub in onward:
            send(to, line, d, sub)

    def core(line, d, part):
        recv("c", line, d, part)

    odd = z % 2
    q0 = z // 2
    turn = 1 - 2 * odd
    quads = [q0, (q0 - turn + 4) % 4, (q0 + turn + 4) % 4, (q0 + 2) % 4]

    def compute(line, phase):
        t = phase * 2 + line
        base = (y + line) % 2 * 1024 + quads[phase] * TILE
        block = g[pl.ds(pl.multiple_of(base, TILE), TILE), :]

        cb[t] = lax.dot_general(
            a[...], block, (((1,), (1,)), ((), ())), preferred_element_type=jnp.float32
        ).astype(jnp.bfloat16)
        for d in (1, 2, 3):
            to = (x + d) % 4
            cp = pltpu.make_async_remote_copy(
                src_ref=cb.at[t, pl.ds(pl.multiple_of(to * CHUNK, CHUNK), CHUNK), :],
                dst_ref=rb.at[t, x], send_sem=s_x.at[t, d], recv_sem=r_x.at[t, x],
                device_id=device(dx=d), device_id_type=MESH,
            )
            cp.start()
            started.append(cp)

    def reduce(line, phase):
        t = phase * 2 + line
        mine = pl.ds(pl.multiple_of(x * CHUNK, CHUNK), CHUNK)
        total = cb[t, mine, :].astype(jnp.float32)
        for d in (1, 2, 3):
            src = (x + d) % 4
            pltpu.make_async_remote_copy(
                src_ref=cb.at[t, mine, :], dst_ref=rb.at[t, src], send_sem=s_x.at[t, d],
                recv_sem=r_x.at[t, src], device_id=device(dx=d), device_id_type=MESH,
            ).wait_recv()
            total += rb[t, src].astype(jnp.float32)
        to = (y + line) % 2 * 4 + quads[phase]

        @pl.when(to == row)
        def _():
            fin[row] = total.astype(jnp.bfloat16)

        @pl.when(to != row)
        def _():
            red[t] = total.astype(jnp.bfloat16)
            final(t, to).start()

    def final(t, to):
        return pltpu.make_async_remote_copy(
            src_ref=red.at[t], dst_ref=fin.at[row], send_sem=s_f.at[t], recv_sem=r_f.at[row],
            device_id=(to, col), device_id_type=MESH,
        )

    send("zp", 0, 0, FULL)
    send("zm", 0, 0, FULL)
    send("y", 0, 0, H1)
    send("y", 0, 0, H0)
    send("c", 0, 0, FULL)

    load_a.wait()
    for i in range(ROWS // BLOCK):
        for k in range(DEPTH // BLOCK):
            keep = sec_ref[col * (ROWS // BLOCK) + i] == sec_ref[row * (DEPTH // BLOCK) + k]
            at = (pl.ds(i * BLOCK, BLOCK), pl.ds(k * BLOCK, BLOCK))
            a[at] = jnp.where(keep, a[at], jnp.zeros((BLOCK, BLOCK), a.dtype))

    hop("y", 1, 0, H1, [("zp", H1), ("zm", H1), ("c", H1)])
    hop("zp", 0, -1, FULL, [("zp", FULL), ("y", H0), ("c", FULL)])
    hop("zm", 0, 1, FULL, [("zm", FULL), ("y", H0), ("c", FULL)])
    hop("y", 1, 0, H0, [("c", H0)])
    core(0, 0, FULL), core(0, -1, FULL), core(0, 1, FULL)
    compute(0, 0)
    hop("zp", 1, -1, H1, [("zp", H1), ("c", H1)])
    hop("zm", 1, 1, H1, [("zm", H1), ("c", H1)])
    hop("y", 1, -1, H0, [("c", H0)])
    hop("y", 1, 1, H0, [("c", H0)])
    reduce(0, 0)
    hop("zp", 0, -2, FULL, [("zp", FULL), ("y", H0), ("c", FULL)])
    hop("zm", 0, 2, FULL, [("zm", FULL), ("y", H0), ("c", FULL)])
    core(1, 0, H1), core(1, 0, H0), core(1, -1, H1), core(1, 1, H1), core(1, -1, H0), core(1, 1, H0)
    compute(1, 0)
    hop("zp", 1, -2, H1, [("zp", H1), ("c", H1)])
    hop("zm", 1, 2, H1, [("zm", H1), ("c", H1)])
    core(0, -2, FULL), core(0, 2, FULL)
    compute(0, 1)
    reduce(1, 0)
    hop("y", 1, -2, H0, [("c", H0)])
    hop("y", 1, 2, H0, [("c", H0)])
    hop("zp", 0, -3, FULL, [("zp", H0), ("y", H0), ("c", FULL)])
    hop("zm", 0, 3, FULL, [("zm", H1), ("y", H0), ("c", FULL)])
    core(1, -2, H1), core(1, 2, H1), core(1, -2, H0), core(1, 2, H0)
    compute(1, 1)
    reduce(0, 1)
    hop("zp", 1, -3, H1, [("zp", H1LO), ("c", H1)])
    hop("zm", 1, 3, H1, [("zm", H1HI), ("c", H1)])
    core(0, -3, FULL), core(0, 3, FULL)
    compute(0, 2)
    reduce(1, 1)
    hop("y", 1, -3, H0, [("c", H0)])
    hop("zp", 0, 4, H0, [("y", H0), ("c", H0)])
    hop("zm", 0, 4, H1, [("c", H1)])
    hop("y", 1, 3, H0, [("c", H0)])
    core(1, -3, H1), core(1, 3, H1), core(1, -3, H0), core(1, 3, H0)
    compute(1, 2)
    hop("zp", 1, 4, H1LO, [("c", H1LO)])
    hop("zm", 1, 4, H1HI, [("c", H1HI)])
    core(0, 4, H0), core(0, 4, H1)
    compute(0, 3)
    reduce(0, 2)
    hop("y", 1, 4, H0, [("c", H0)])
    core(1, 4, H1LO), core(1, 4, H1HI), core(1, 4, H0)
    compute(1, 3)
    reduce(1, 2)
    reduce(0, 3)
    reduce(1, 3)

    for h, d in [(h, d) for d in range(4) for h in (0, 1) if (h, d) != (0, 0)]:
        src = (yh + h) % 2 * 4 + (x + d) % 4
        pltpu.make_async_remote_copy(
            src_ref=red.at[0], dst_ref=fin.at[src], send_sem=s_f.at[0], recv_sem=r_f.at[src],
            device_id=device(dyh=h, dx=d), device_id_type=MESH,
        ).wait_recv()
    for part in range(4):
        out_ref[part * CHUNK : (part + 1) * CHUNK, :] = (
            fin[part].astype(jnp.float32) + fin[4 + part].astype(jnp.float32)
        ).astype(out_ref.dtype)

    for cp in started:
        cp.wait_send()
    for line in (0, 1):
        for phase in range(4):
            to = (y + line) % 2 * 4 + quads[phase]

            @pl.when(to != row)
            def _():
                final(phase * 2 + line, to).wait_send()


def body(sectors, environment, wavefunction):
    dma = pltpu.SemaphoreType.DMA
    pairs = []
    for link in ("zp", "zm", "y", "c"):
        pairs += [dma((len(LINKS[link]),)), dma((len(LINKS[link]),))]
    return pl.pallas_call(
        kernel,
        out_shape=jax.ShapeDtypeStruct((ROWS, TILE), jnp.bfloat16),
        in_specs=[
            pl.BlockSpec(memory_space=pltpu.SMEM),
            pl.BlockSpec(memory_space=pl.ANY),
            pl.BlockSpec(memory_space=pl.ANY),
        ],
        out_specs=pl.BlockSpec(memory_space=pltpu.VMEM),
        scratch_shapes=[
            pltpu.VMEM((ROWS, DEPTH), jnp.bfloat16),
            pltpu.VMEM((32 * ITEM, DEPTH), jnp.bfloat16),
            pltpu.VMEM((8, ROWS, TILE), jnp.bfloat16),
            pltpu.VMEM((8, 4, CHUNK, TILE), jnp.bfloat16),
            pltpu.VMEM((8, CHUNK, TILE), jnp.bfloat16),
            pltpu.VMEM((8, CHUNK, TILE), jnp.bfloat16),
            *pairs,
            dma((8, 4)), dma((8, 4)), dma((8,)), dma((8,)), dma((2,)),
        ],
        compiler_params=pltpu.CompilerParams(
            collective_id=0, has_side_effects=True, vmem_limit_bytes=56 << 20
        ),
    )(sectors, environment, wavefunction.T)


def solution(mesh):
    placed = (P(), P("col", "row"), P("row", "col"))
    return jax.shard_map(
        body, mesh=mesh, in_specs=placed, out_specs=P("col", "row"), check_vma=False
    )
```

```python
import jax
import jax.numpy as jnp
from jax import lax
from jax.experimental import pallas as pl
from jax.experimental.pallas import tpu as pltpu
from jax.sharding import PartitionSpec as P

MESH = pl.DeviceIdType.MESH
BLOCK = 256
ITEM = 64
PAIR = 2 * ITEM
ROWS = 768
DEPTH = 3072
HALF = DEPTH // 2
TILE = 256
CHUNK = ROWS // 4

H0 = (0, ITEM, 0, HALF)
H1 = (0, ITEM, HALF, HALF)
LO = (0, ITEM // 2, HALF, HALF)
HI = (ITEM // 2, ITEM // 2, HALF, HALF)

DIST = [0, -1, 1, -2, 2, -3, 3, 4]

ZP = [(0, -d, h) for d in range(3) for h in (H0, H1)] + [(1, -d, H1) for d in range(3)] + [(0, -3, H0), (1, -3, LO)]
ZM = [(0, d, h) for d in range(3) for h in (H0, H1)] + [(1, d, H1) for d in range(3)] + [(0, 3, H1), (1, 3, HI)]
YY = [(0, 0, H1)] + [(0, d, H0) for d in DIST]
CC = [(line, d, h) for line in (0, 1) for d in DIST for h in (H0, H1) if (line, d, h) != (1, 4, H1)]
CC += [(1, 4, LO), (1, 4, HI)]
LINKS = {"zp": ZP, "zm": ZM, "y": YY, "c": CC}

ORDER = [
    ("mm", 0, 0),
    ("zp", 0, -1, H0),
    ("zm", 0, 1, H0),
    ("y", 1, 0, H1),
    ("ra", 0, 0),
    ("zp", 0, -1, H1),
    ("zm", 0, 1, H1),
    ("y", 1, 0, H0),
    ("mm", 0, -1),
    ("mm", 0, 1),
    ("y", 1, -1, H0),
    ("zp", 0, -2, H0),
    ("zm", 0, 2, H0),
    ("mm", 1, 0),
    ("ra", 0, -1),
    ("zp", 1, -1, H1),
    ("zm", 1, 1, H1),
    ("y", 1, 1, H0),
    ("ra", 0, 1),
    ("mm", 1, -1),
    ("mm", 1, 1),
    ("zp", 0, -2, H1),
    ("zm", 0, 2, H1),
    ("y", 1, -2, H0),
    ("ra", 1, 0),
    ("mm", 0, -2),
    ("mm", 0, 2),
    ("zp", 0, -3, H0),
    ("zm", 0, 3, H0),
    ("y", 1, 2, H0),
    ("ra", 1, -1),
    ("ra", 1, 1),
    ("rb", 0),
    ("ra", 0, -2),
    ("zp", 1, -2, H1),
    ("zm", 1, 2, H1),
    ("mm", 1, -2),
    ("y", 1, -3, H0),
    ("ra", 0, 2),
    ("mm", 1, 2),
    ("zp", 0, -3, H1),
    ("zm", 0, 3, H1),
    ("mm", 0, -3),
    ("y", 1, 3, H0),
    ("ra", 1, -2),
    ("rb", -1),
    ("zm", 1, 3, H1),
    ("zp", 0, 4, H0),
    ("rb", 1),
    ("mm", 0, 3),
    ("ra", 1, 2),
    ("mm", 1, 3),
    ("rb", -2),
    ("ra", 0, -3),
    ("zp", 1, -3, H1),
    ("zm", 0, 4, H1),
    ("mm", 1, -3),
    ("y", 1, 4, H0),
    ("zm", 1, 4, HI),
    ("ra", 0, 3),
    ("rb", 2),
    ("mm", 0, 4),
    ("zp", 1, 4, LO),
    ("ra", 1, 3),
    ("mm", 1, 4),
    ("ra", 1, -3),
    ("rb", 3),
    ("ra", 0, 4),
    ("rb", -3),
    ("ra", 1, 4),
    ("rb", 4),
]


def onward(link, line, d, part):
    to = [("c", part)]
    if link == "y":
        return to + ([("zp", part), ("zm", part)] if part == H1 else [])
    if line == 0 and part == H0:
        to.append(("y", part))
    if abs(d) < 3:
        to.insert(0, (link, part))
    elif abs(d) == 3 and line == 1:
        to.insert(0, (link, LO if link == "zp" else HI))
    elif abs(d) == 3 and part == (H0 if link == "zp" else H1):
        to.insert(0, (link, part))
    return to


def kernel(sec_ref, env_ref, wave_ref, out_ref, a, g, cb, rb, keep, red, yr, done, fin,
           s_zp, r_zp, s_zm, r_zm, s_y, r_y, s_c, r_c, s_x, r_x, s_h, r_h, s_f, r_f, local):
    row, col = lax.axis_index("row"), lax.axis_index("col")
    yh, x = row // 4, row % 4
    y, z, c = col // 16, (col // 2) % 8, col % 2

    def device(dyh=0, dx=0, dy=0, dz=0, dc=0):
        return (
            (yh + dyh) % 2 * 4 + (x + dx) % 4,
            (y + dy) % 2 * 16 + (z + dz + 8) % 8 * 2 + (c + dc) % 2,
        )

    load_a = pltpu.make_async_copy(env_ref, a, local.at[0])
    own = pl.ds(pl.multiple_of(col * ITEM, ITEM), ITEM)
    load_b = pltpu.make_async_copy(wave_ref, g.at[own, :], local.at[1])
    load_b.start()
    load_a.start()

    barrier = pltpu.get_barrier_semaphore()
    greet = [device(dz=1), device(dz=-1), device(dy=1), device(dc=1), device(dyh=1)]
    greet += [device(dx=d) for d in (1, 2, 3)]
    for peer in greet:
        pl.semaphore_signal(barrier, inc=1, device_id=peer, device_id_type=MESH)
    load_b.wait()
    pl.semaphore_wait(barrier, len(greet))

    sems = {"zp": (s_zp, r_zp), "zm": (s_zm, r_zm), "y": (s_y, r_y), "c": (s_c, r_c)}
    peers = {"zp": device(dz=1), "zm": device(dz=-1), "y": device(dy=1), "c": device(dc=1)}
    moves = {"zp": (0, -1, 0), "zm": (0, 1, 0), "y": (1, 0, 0), "c": (0, 0, 1)}
    started = []

    def piece(line, d, part, parity):
        r0, nr, k0, nk = part
        j = (y + line) % 2 * 16 + (z + d + 8) % 8 * 2 + (c + parity) % 2
        return g.at[pl.ds(pl.multiple_of(j * ITEM + r0, 32), nr), pl.ds(k0, nk)]

    def copy(link, ref, i):
        return pltpu.make_async_remote_copy(
            src_ref=ref, dst_ref=ref, send_sem=sems[link][0].at[i], recv_sem=sems[link][1].at[i],
            device_id=peers[link], device_id_type=MESH,
        )

    def send(link, line, d, part):
        cp = copy(link, piece(line, d, part, 0), LINKS[link].index((line, d, part)))
        cp.start()
        started.append(cp)

    def recv(link, line, d, part):
        dl, dz, dc = moves[link]
        sd = d - dz
        sd = {-4: 4, 5: -3, -5: 3}.get(sd, sd)
        i = LINKS[link].index(((line + dl) % 2, sd, part))
        copy(link, piece(line, d, part, dc), i).wait_recv()

    def multiply(line, d):
        for part in (H0, LO, HI) if (line, d) == (1, 4) else (H0, H1):
            recv("c", line, d, part)
        t = DIST.index(d) * 2 + line
        base = (y + line) % 2 * (16 * ITEM) + (z + d + 8) % 8 * PAIR
        block = g[pl.ds(pl.multiple_of(base, PAIR), PAIR), :]
        cb[t] = lax.dot_general(
            a[...], block, (((1,), (1,)), ((), ())), preferred_element_type=jnp.float32
        ).astype(jnp.bfloat16)
        for dx in (2, 1, 3):
            cp = share(t, dx, (x + dx) % 4, x)
            cp.start()
            started.append(cp)

    def share(t, dx, chunk, slot):
        return pltpu.make_async_remote_copy(
            src_ref=cb.at[t, pl.ds(pl.multiple_of(chunk * CHUNK, CHUNK), CHUNK), :],
            dst_ref=rb.at[t, slot], send_sem=s_x.at[t, dx], recv_sem=r_x.at[t, slot],
            device_id=device(dx=dx), device_id_type=MESH,
        )

    def over_y(i):
        return pltpu.make_async_remote_copy(
            src_ref=red.at[i], dst_ref=yr.at[i], send_sem=s_h.at[i], recv_sem=r_h.at[i],
            device_id=device(dyh=1), device_id_type=MESH,
        )

    def add_x(line, d):
        i = DIST.index(d)
        t = i * 2 + line
        total = cb[t, pl.ds(pl.multiple_of(x * CHUNK, CHUNK), CHUNK), :].astype(jnp.float32)
        for dx in (1, 3, 2):
            src = (x + dx) % 4
            share(t, dx, x, src).wait_recv()
            total += rb[t, src].astype(jnp.float32)
        stays = (y + line) % 2 == yh

        @pl.when(stays)
        def _():
            keep[i] = total

        @pl.when(jnp.logical_not(stays))
        def _():
            red[i] = total.astype(jnp.bfloat16)
            over_y(i).start()

    def final(i, half, to):
        return pltpu.make_async_remote_copy(
            src_ref=done.at[i], dst_ref=fin.at[x, half], send_sem=s_f.at[i], recv_sem=r_f.at[x],
            device_id=(yh * 4 + to, col), device_id_type=MESH,
        )

    def add_y(d):
        i = DIST.index(d)
        over_y(i).wait_recv()
        total = (keep[i] + yr[i].astype(jnp.float32)).astype(jnp.bfloat16)
        at = (z + d + 8) % 8
        half, to = at % 2, at // 2

        @pl.when(to == x)
        def _():
            fin[x, half] = total

        @pl.when(to != x)
        def _():
            done[i] = total
            final(i, half, to).start()

    for part in (H0, H1):
        send("zp", 0, 0, part)
        send("zm", 0, 0, part)
    for part in (H1, H0):
        send("y", 0, 0, part)
    for part in (H0, H1):
        send("c", 0, 0, part)

    load_a.wait()
    for i in range(ROWS // BLOCK):
        for k in range(DEPTH // BLOCK):
            same = sec_ref[col * (ROWS // BLOCK) + i] == sec_ref[row * (DEPTH // BLOCK) + k]
            at = (pl.ds(i * BLOCK, BLOCK), pl.ds(k * BLOCK, BLOCK))
            a[at] = jnp.where(same, a[at], jnp.zeros((BLOCK, BLOCK), a.dtype))

    steps = {"mm": multiply, "ra": add_x, "rb": add_y}
    for name, *args in ORDER:
        if name in steps:
            steps[name](*args)
        else:
            recv(name, *args)
            line, d, _ = args
            for to, part in onward(name, *args):
                send(to, line, d, part)

    for dx in (1, 2, 3):
        src = (x + dx) % 4
        pltpu.make_async_remote_copy(
            src_ref=fin.at[x], dst_ref=fin.at[src], send_sem=s_f.at[0], recv_sem=r_f.at[src],
            device_id=device(dx=dx), device_id_type=MESH,
        ).wait_recv()
    for part in range(4):
        for half in (0, 1):
            at = (pl.ds(part * CHUNK, CHUNK), pl.ds(half * PAIR, PAIR))
            out_ref[at] = fin[part, half]

    for cp in started:
        cp.wait_send()
    for i, d in enumerate(DIST):
        over_y(i).wait_send()
        at = (z + d + 8) % 8

        @pl.when(at // 2 != x)
        def _():
            final(i, at % 2, at // 2).wait_send()


def body(sectors, environment, wavefunction):
    dma = pltpu.SemaphoreType.DMA
    pairs = []
    for link in ("zp", "zm", "y", "c"):
        pairs += [dma((len(LINKS[link]),)), dma((len(LINKS[link]),))]
    return pl.pallas_call(
        kernel,
        out_shape=jax.ShapeDtypeStruct((ROWS, TILE), jnp.bfloat16),
        in_specs=[
            pl.BlockSpec(memory_space=pltpu.SMEM),
            pl.BlockSpec(memory_space=pl.ANY),
            pl.BlockSpec(memory_space=pl.ANY),
        ],
        out_specs=pl.BlockSpec(memory_space=pltpu.VMEM),
        scratch_shapes=[
            pltpu.VMEM((ROWS, DEPTH), jnp.bfloat16),
            pltpu.VMEM((32 * ITEM, DEPTH), jnp.bfloat16),
            pltpu.VMEM((16, ROWS, PAIR), jnp.bfloat16),
            pltpu.VMEM((16, 4, CHUNK, PAIR), jnp.bfloat16),
            pltpu.VMEM((8, CHUNK, PAIR), jnp.float32),
            pltpu.VMEM((8, CHUNK, PAIR), jnp.bfloat16),
            pltpu.VMEM((8, CHUNK, PAIR), jnp.bfloat16),
            pltpu.VMEM((8, CHUNK, PAIR), jnp.bfloat16),
            pltpu.VMEM((4, 2, CHUNK, PAIR), jnp.bfloat16),
            *pairs,
            dma((16, 4)), dma((16, 4)), dma((8,)), dma((8,)), dma((8,)), dma((4,)), dma((2,)),
        ],
        compiler_params=pltpu.CompilerParams(
            collective_id=0, has_side_effects=True, vmem_limit_bytes=56 << 20
        ),
    )(sectors, environment, wavefunction.T)


def solution(mesh):
    placed = (P(), P("col", "row"), P("row", "col"))
    return jax.shard_map(
        body, mesh=mesh, in_specs=placed, out_specs=P("col", "row"), check_vma=False
    )
```

```python
import jax
import jax.numpy as jnp
from jax import lax
from jax.experimental import pallas as pl
from jax.experimental.pallas import tpu as pltpu
from jax.sharding import PartitionSpec as P

MESH = pl.DeviceIdType.MESH
BLOCK = 256
ITEM = 64
PAIR = 2 * ITEM
ROWS = 768
DEPTH = 3072
HALF = DEPTH // 2
TILE = 256
CHUNK = ROWS // 4
STEP = 256

H0 = (0, ITEM, 0, HALF)
H1 = (0, ITEM, HALF, HALF)
LO = (0, ITEM // 2, HALF, HALF)
HI = (ITEM // 2, ITEM // 2, HALF, HALF)

DIST = [0, -1, 1, -2, 2, -3, 3, 4]

ZP = [(0, -d, h) for d in range(3) for h in (H0, H1)] + [(1, -d, H1) for d in range(3)] + [(0, -3, H0), (1, -3, LO)]
ZM = [(0, d, h) for d in range(3) for h in (H0, H1)] + [(1, d, H1) for d in range(3)] + [(0, 3, H1), (1, 3, HI)]
YY = [(0, 0, H1)] + [(0, d, H0) for d in DIST]
CC = [(line, d, h) for line in (0, 1) for d in DIST for h in (H0, H1) if (line, d, h) != (1, 4, H1)]
CC += [(1, 4, LO), (1, 4, HI)]
LINKS = {"zp": ZP, "zm": ZM, "y": YY, "c": CC}

ORDER = [
    ("mm", 0, 0),
    ("zp", 0, -1, H0),
    ("zm", 0, 1, H0),
    ("y", 1, 0, H1),
    ("ra", 0, 0),
    ("zp", 0, -1, H1),
    ("zm", 0, 1, H1),
    ("y", 1, 0, H0),
    ("mm", 0, -1),
    ("mm", 0, 1),
    ("y", 1, -1, H0),
    ("zp", 0, -2, H0),
    ("zm", 0, 2, H0),
    ("mm", 1, 0),
    ("zp", 1, -1, H1),
    ("zm", 1, 1, H1),
    ("y", 1, 1, H0),
    ("ra", 0, -1),
    ("mm", 1, -1),
    ("ra", 0, 1),
    ("mm", 1, 1),
    ("zp", 0, -2, H1),
    ("zm", 0, 2, H1),
    ("y", 1, -2, H0),
    ("ra", 1, 0),
    ("mm", 0, -2),
    ("zp", 0, -3, H0),
    ("zm", 0, 3, H0),
    ("ra", 1, -1),
    ("y", 1, 2, H0),
    ("mm", 0, 2),
    ("ra", 1, 1),
    ("rb", 0),
    ("zp", 1, -2, H1),
    ("zm", 1, 2, H1),
    ("ra", 0, -2),
    ("mm", 1, -2),
    ("y", 1, -3, H0),
    ("mm", 1, 2),
    ("zp", 0, -3, H1),
    ("zm", 0, 3, H1),
    ("ra", 0, 2),
    ("y", 1, 3, H0),
    ("mm", 0, -3),
    ("rb", -1),
    ("zm", 1, 3, H1),
    ("zp", 0, 4, H0),
    ("rb", 1),
    ("ra", 1, -2),
    ("mm", 0, 3),
    ("ra", 1, 2),
    ("mm", 1, 3),
    ("zp", 1, -3, H1),
    ("zm", 0, 4, H1),
    ("ra", 0, -3),
    ("mm", 1, -3),
    ("zm", 1, 4, HI),
    ("y", 1, 4, H0),
    ("mm", 0, 4),
    ("zp", 1, 4, LO),
    ("rb", -2),
    ("rb", 2),
    ("ra", 0, 3),
    ("ra", 1, 3),
    ("mm", 1, 4),
    ("ra", 1, -3),
    ("rb", 3),
    ("ra", 0, 4),
    ("rb", -3),
    ("ra", 1, 4),
    ("rb", 4),
]


def onward(link, line, d, part):
    to = [("c", part)]
    if link == "y":
        return to + ([("zp", part), ("zm", part)] if part == H1 else [])
    if line == 0 and part == H0:
        to.append(("y", part))
    if abs(d) < 3:
        to.insert(0, (link, part))
    elif abs(d) == 3 and line == 1:
        to.insert(0, (link, LO if link == "zp" else HI))
    elif abs(d) == 3 and part == (H0 if link == "zp" else H1):
        to.insert(0, (link, part))
    return to


def kernel(sec_ref, env_ref, wave_ref, out_ref, a, g, cb, rb, keep, red, yr, done, fin,
           s_zp, r_zp, s_zm, r_zm, s_y, r_y, s_c, r_c, s_x, r_x, s_h, r_h, s_f, r_f, local):
    row, col = lax.axis_index("row"), lax.axis_index("col")
    yh, x = row // 4, row % 4
    y, z, c = col // 16, (col // 2) % 8, col % 2

    def device(dyh=0, dx=0, dy=0, dz=0, dc=0):
        return (
            (yh + dyh) % 2 * 4 + (x + dx) % 4,
            (y + dy) % 2 * 16 + (z + dz + 8) % 8 * 2 + (c + dc) % 2,
        )

    load_a = pltpu.make_async_copy(env_ref, a, local.at[0])
    own = pl.ds(pl.multiple_of(col * ITEM, ITEM), ITEM)
    load_b = pltpu.make_async_copy(wave_ref, g.at[own, :], local.at[1])
    load_b.start()
    load_a.start()

    barrier = pltpu.get_barrier_semaphore()
    greet = [device(dz=1), device(dz=-1), device(dy=1), device(dc=1), device(dyh=1)]
    greet += [device(dx=d) for d in (1, 2, 3)]
    for peer in greet:
        pl.semaphore_signal(barrier, inc=1, device_id=peer, device_id_type=MESH)
    load_b.wait()
    pl.semaphore_wait(barrier, len(greet))

    sems = {"zp": (s_zp, r_zp), "zm": (s_zm, r_zm), "y": (s_y, r_y), "c": (s_c, r_c)}
    peers = {"zp": device(dz=1), "zm": device(dz=-1), "y": device(dy=1), "c": device(dc=1)}
    moves = {"zp": (0, -1, 0), "zm": (0, 1, 0), "y": (1, 0, 0), "c": (0, 0, 1)}
    started = []

    def piece(line, d, part, parity):
        r0, nr, k0, nk = part
        j = (y + line) % 2 * 16 + (z + d + 8) % 8 * 2 + (c + parity) % 2
        return g.at[pl.ds(pl.multiple_of(j * ITEM + r0, 32), nr), pl.ds(k0, nk)]

    def copy(link, ref, i):
        return pltpu.make_async_remote_copy(
            src_ref=ref, dst_ref=ref, send_sem=sems[link][0].at[i], recv_sem=sems[link][1].at[i],
            device_id=peers[link], device_id_type=MESH,
        )

    def send(link, line, d, part):
        cp = copy(link, piece(line, d, part, 0), LINKS[link].index((line, d, part)))
        cp.start()
        started.append(cp)

    def recv(link, line, d, part):
        dl, dz, dc = moves[link]
        sd = d - dz
        sd = {-4: 4, 5: -3, -5: 3}.get(sd, sd)
        i = LINKS[link].index(((line + dl) % 2, sd, part))
        copy(link, piece(line, d, part, dc), i).wait_recv()

    def multiply(line, d):
        for part in (H0, LO, HI) if (line, d) == (1, 4) else (H0, H1):
            recv("c", line, d, part)
        t = DIST.index(d) * 2 + line
        base = (y + line) % 2 * (16 * ITEM) + (z + d + 8) % 8 * PAIR
        block = pl.ds(pl.multiple_of(base, PAIR), PAIR)

        step = CHUNK if d == 4 else STEP

        def rows(m, _):
            far = 2 - m + m // 2 * (3 - 2 * (m % 2))
            at = (x + far) % 4 if d == 4 else m
            at = pl.ds(pl.multiple_of(at * step, step), step)
            cb[t, at, :] = lax.dot_general(
                a[at, :], g[block, :], (((1,), (1,)), ((), ())), preferred_element_type=jnp.float32
            ).astype(jnp.bfloat16)
            if d == 4:

                @pl.when(far != 0)
                def _():
                    share(t, far, (x + far) % 4, x).start()

            return 0

        lax.fori_loop(0, ROWS // step, rows, 0)
        for dx in (2, 1, 3):
            cp = share(t, dx, (x + dx) % 4, x)
            if d != 4:
                cp.start()
            started.append(cp)

    def share(t, dx, chunk, slot):
        return pltpu.make_async_remote_copy(
            src_ref=cb.at[t, pl.ds(pl.multiple_of(chunk * CHUNK, CHUNK), CHUNK), :],
            dst_ref=rb.at[t, slot], send_sem=s_x.at[t, dx], recv_sem=r_x.at[t, slot],
            device_id=device(dx=dx), device_id_type=MESH,
        )

    def over_y(i):
        return pltpu.make_async_remote_copy(
            src_ref=red.at[i], dst_ref=yr.at[i], send_sem=s_h.at[i], recv_sem=r_h.at[i],
            device_id=device(dyh=1), device_id_type=MESH,
        )

    def add_x(line, d):
        i = DIST.index(d)
        t = i * 2 + line
        total = cb[t, pl.ds(pl.multiple_of(x * CHUNK, CHUNK), CHUNK), :].astype(jnp.float32)
        for dx in (1, 3, 2):
            src = (x + dx) % 4
            share(t, dx, x, src).wait_recv()
            total += rb[t, src].astype(jnp.float32)
        stays = (y + line) % 2 == yh

        @pl.when(stays)
        def _():
            keep[i] = total

        @pl.when(jnp.logical_not(stays))
        def _():
            red[i] = total.astype(jnp.bfloat16)
            over_y(i).start()

    def final(i, half, to):
        return pltpu.make_async_remote_copy(
            src_ref=done.at[i], dst_ref=fin.at[x, half], send_sem=s_f.at[i], recv_sem=r_f.at[x],
            device_id=(yh * 4 + to, col), device_id_type=MESH,
        )

    def add_y(d):
        i = DIST.index(d)
        over_y(i).wait_recv()
        total = (keep[i] + yr[i].astype(jnp.float32)).astype(jnp.bfloat16)
        at = (z + d + 8) % 8
        half, to = at % 2, at // 2

        @pl.when(to == x)
        def _():
            fin[x, half] = total

        @pl.when(to != x)
        def _():
            done[i] = total
            final(i, half, to).start()

    for part in (H0, H1):
        send("zp", 0, 0, part)
        send("zm", 0, 0, part)
    for part in (H1, H0):
        send("y", 0, 0, part)
    for part in (H0, H1):
        send("c", 0, 0, part)

    load_a.wait()
    for i in range(ROWS // BLOCK):
        for k in range(DEPTH // BLOCK):
            same = sec_ref[col * (ROWS // BLOCK) + i] == sec_ref[row * (DEPTH // BLOCK) + k]
            at = (pl.ds(i * BLOCK, BLOCK), pl.ds(k * BLOCK, BLOCK))
            a[at] = jnp.where(same, a[at], jnp.zeros((BLOCK, BLOCK), a.dtype))

    steps = {"mm": multiply, "ra": add_x, "rb": add_y}
    for name, *args in ORDER:
        if name in steps:
            steps[name](*args)
        else:
            recv(name, *args)
            line, d, _ = args
            for to, part in onward(name, *args):
                send(to, line, d, part)

    for dx in (1, 2, 3):
        src = (x + dx) % 4
        pltpu.make_async_remote_copy(
            src_ref=fin.at[x], dst_ref=fin.at[src], send_sem=s_f.at[0], recv_sem=r_f.at[src],
            device_id=device(dx=dx), device_id_type=MESH,
        ).wait_recv()
    for part in range(4):
        for half in (0, 1):
            at = (pl.ds(part * CHUNK, CHUNK), pl.ds(half * PAIR, PAIR))
            out_ref[at] = fin[part, half]

    for cp in started:
        cp.wait_send()
    for i, d in enumerate(DIST):
        over_y(i).wait_send()
        at = (z + d + 8) % 8

        @pl.when(at // 2 != x)
        def _():
            final(i, at % 2, at // 2).wait_send()


def body(sectors, environment, wavefunction):
    dma = pltpu.SemaphoreType.DMA
    pairs = []
    for link in ("zp", "zm", "y", "c"):
        pairs += [dma((len(LINKS[link]),)), dma((len(LINKS[link]),))]
    return pl.pallas_call(
        kernel,
        out_shape=pltpu.VMEM((ROWS, TILE), jnp.bfloat16),
        in_specs=[
            pl.BlockSpec(memory_space=pltpu.SMEM),
            pl.BlockSpec(memory_space=pl.ANY),
            pl.BlockSpec(memory_space=pl.ANY),
        ],
        out_specs=pl.BlockSpec(memory_space=pltpu.VMEM),
        scratch_shapes=[
            pltpu.VMEM((ROWS, DEPTH), jnp.bfloat16),
            pltpu.VMEM((32 * ITEM, DEPTH), jnp.bfloat16),
            pltpu.VMEM((16, ROWS, PAIR), jnp.bfloat16),
            pltpu.VMEM((16, 4, CHUNK, PAIR), jnp.bfloat16),
            pltpu.VMEM((8, CHUNK, PAIR), jnp.float32),
            pltpu.VMEM((8, CHUNK, PAIR), jnp.bfloat16),
            pltpu.VMEM((8, CHUNK, PAIR), jnp.bfloat16),
            pltpu.VMEM((8, CHUNK, PAIR), jnp.bfloat16),
            pltpu.VMEM((4, 2, CHUNK, PAIR), jnp.bfloat16),
            *pairs,
            dma((16, 4)), dma((16, 4)), dma((8,)), dma((8,)), dma((8,)), dma((4,)), dma((2,)),
        ],
        compiler_params=pltpu.CompilerParams(
            collective_id=0, has_side_effects=True, vmem_limit_bytes=56 << 20
        ),
    )(sectors, environment, wavefunction.T)


def solution(mesh):
    placed = (P(), P("col", "row"), P("row", "col"))
    return jax.shard_map(
        body, mesh=mesh, in_specs=placed, out_specs=P("col", "row"), check_vma=False
    )
```

```python
import jax
import jax.numpy as jnp
from jax import lax
from jax.experimental import pallas as pl
from jax.experimental.pallas import tpu as pltpu
from jax.sharding import PartitionSpec as P

MESH = pl.DeviceIdType.MESH
BLOCK = 256
ITEM = 64
PAIR = 2 * ITEM
ROWS = 768
DEPTH = 3072
HALF = 1664
TILE = 256
CHUNK = ROWS // 4
STEP = 256

H0 = (0, ITEM, 0, HALF)
H1 = (0, ITEM, HALF, DEPTH - HALF)
LO = (0, ITEM // 2, HALF, DEPTH - HALF)
HI = (ITEM // 2, ITEM // 2, HALF, DEPTH - HALF)

DIST = [0, -1, 1, -2, 2, -3, 3, 4]

ZP = [(0, -d, h) for d in range(3) for h in (H0, H1)] + [(1, -d, H1) for d in range(3)] + [(0, -3, H0), (1, -3, LO)]
ZM = [(0, d, h) for d in range(3) for h in (H0, H1)] + [(1, d, H1) for d in range(3)] + [(0, 3, H1), (1, 3, HI)]
YY = [(0, 0, H1)] + [(0, d, H0) for d in DIST]
CC = [(line, d, h) for line in (0, 1) for d in DIST for h in (H0, H1) if (line, d, h) != (1, 4, H1)]
CC += [(1, 4, LO), (1, 4, HI)]
LINKS = {"zp": ZP, "zm": ZM, "y": YY, "c": CC}

ORDER = [
    ("mm", 0, 0),
    ("y", 1, 0, H1),
    ("zp", 0, -1, H0),
    ("zm", 0, 1, H0),
    ("ra", 0, 0),
    ("zp", 0, -1, H1),
    ("zm", 0, 1, H1),
    ("y", 1, 0, H0),
    ("mm", 0, -1),
    ("zp", 1, -1, H1),
    ("zm", 1, 1, H1),
    ("mm", 0, 1),
    ("y", 1, -1, H0),
    ("mm", 1, 0),
    ("mm", 1, -1),
    ("y", 1, 1, H0),
    ("zp", 0, -2, H0),
    ("zm", 0, 2, H0),
    ("ra", 0, -1),
    ("mm", 1, 1),
    ("ra", 1, 0),
    ("zp", 0, -2, H1),
    ("zm", 0, 2, H1),
    ("ra", 0, 1),
    ("mm", 0, -2),
    ("y", 1, -2, H0),
    ("zm", 1, 2, H1),
    ("mm", 0, 2),
    ("ra", 1, -1),
    ("ra", 1, 1),
    ("y", 1, 2, H0),
    ("zm", 0, 3, H0),
    ("zp", 0, -3, H0),
    ("zp", 1, -2, H1),
    ("mm", 1, 2),
    ("zp", 0, -3, H1),
    ("zm", 0, 3, H1),
    ("mm", 1, -2),
    ("mm", 0, -3),
    ("y", 1, 3, H0),
    ("zm", 1, 3, H1),
    ("mm", 0, 3),
    ("zp", 0, 4, H0),
    ("mm", 1, 3),
    ("zm", 0, 4, H1),
    ("y", 1, -3, H0),
    ("zp", 1, -3, H1),
    ("mm", 0, 4),
    ("zm", 1, 4, HI),
    ("mm", 1, -3),
    ("y", 1, 4, H0),
    ("zp", 1, 4, LO),
    ("ra", 0, -2),
    ("ra", 1, 2),
    ("ra", 1, -2),
    ("ra", 0, -3),
    ("mm", 1, 4),
    ("ra", 0, 3),
    ("ra", 0, 4),
    ("rb", -1),
    ("rb", 1),
    ("rb", -2),
    ("ra", 1, -3),
    ("ra", 1, 3),
    ("ra", 0, 2),
    ("rb", 0),
    ("ra", 1, 4),
    ("rb", -3),
    ("rb", 3),
    ("rb", 2),
    ("rb", 4),
]


def onward(link, line, d, part):
    to = [("c", part)]
    if link == "y":
        return to + ([("zp", part), ("zm", part)] if part == H1 else [])
    if line == 0 and part == H0:
        to.append(("y", part))
    if abs(d) < 3:
        to.insert(0, (link, part))
    elif abs(d) == 3 and line == 1:
        to.insert(0, (link, LO if link == "zp" else HI))
    elif abs(d) == 3 and part == (H0 if link == "zp" else H1):
        to.insert(0, (link, part))
    return to


def kernel(sec_ref, env_ref, wave_ref, out_ref, a, g, cb, rb, keep, red, yr, done, fin,
           s_zp, r_zp, s_zm, r_zm, s_y, r_y, s_c, r_c, s_x, r_x, s_h, r_h, s_f, r_f, local):
    row, col = lax.axis_index("row"), lax.axis_index("col")
    yh, x = row // 4, row % 4
    y, z, c = col // 16, (col // 2) % 8, col % 2

    def device(dyh=0, dx=0, dy=0, dz=0, dc=0):
        return (
            (yh + dyh) % 2 * 4 + (x + dx) % 4,
            (y + dy) % 2 * 16 + (z + dz + 8) % 8 * 2 + (c + dc) % 2,
        )

    load_a = pltpu.make_async_copy(env_ref, a, local.at[0])
    own = pl.ds(pl.multiple_of(col * ITEM, ITEM), ITEM)
    load_b = pltpu.make_async_copy(wave_ref, g.at[own, :], local.at[1])
    load_b.start()
    load_a.start()

    barrier = pltpu.get_barrier_semaphore()
    greet = [device(dz=1), device(dz=-1), device(dy=1), device(dc=1), device(dyh=1)]
    greet += [device(dx=d) for d in (1, 2, 3)]
    for peer in greet:
        pl.semaphore_signal(barrier, inc=1, device_id=peer, device_id_type=MESH)
    load_b.wait()
    pl.semaphore_wait(barrier, len(greet))

    sems = {"zp": (s_zp, r_zp), "zm": (s_zm, r_zm), "y": (s_y, r_y), "c": (s_c, r_c)}
    peers = {"zp": device(dz=1), "zm": device(dz=-1), "y": device(dy=1), "c": device(dc=1)}
    moves = {"zp": (0, -1, 0), "zm": (0, 1, 0), "y": (1, 0, 0), "c": (0, 0, 1)}
    started = []

    def piece(line, d, part, parity):
        r0, nr, k0, nk = part
        j = (y + line) % 2 * 16 + (z + d + 8) % 8 * 2 + (c + parity) % 2
        return g.at[pl.ds(pl.multiple_of(j * ITEM + r0, 32), nr), pl.ds(k0, nk)]

    def copy(link, ref, i):
        return pltpu.make_async_remote_copy(
            src_ref=ref, dst_ref=ref, send_sem=sems[link][0].at[i], recv_sem=sems[link][1].at[i],
            device_id=peers[link], device_id_type=MESH,
        )

    def send(link, line, d, part):
        cp = copy(link, piece(line, d, part, 0), LINKS[link].index((line, d, part)))
        cp.start()
        started.append(cp)

    def recv(link, line, d, part):
        dl, dz, dc = moves[link]
        sd = d - dz
        sd = {-4: 4, 5: -3, -5: 3}.get(sd, sd)
        i = LINKS[link].index(((line + dl) % 2, sd, part))
        copy(link, piece(line, d, part, dc), i).wait_recv()

    def multiply(line, d):
        for part in (H0, LO, HI) if (line, d) == (1, 4) else (H0, H1):
            recv("c", line, d, part)
        t = DIST.index(d) * 2 + line
        base = (y + line) % 2 * (16 * ITEM) + (z + d + 8) % 8 * PAIR
        block = pl.ds(pl.multiple_of(base, PAIR), PAIR)

        step = CHUNK if d == 4 else STEP

        def rows(m, _):
            far = 2 - m + m // 2 * (3 - 2 * (m % 2))
            at = (x + far) % 4 if d == 4 else m
            at = pl.ds(pl.multiple_of(at * step, step), step)
            cb[t, at, :] = lax.dot_general(
                a[at, :], g[block, :], (((1,), (1,)), ((), ())), preferred_element_type=jnp.float32
            ).astype(jnp.bfloat16)
            if d == 4:

                @pl.when(far != 0)
                def _():
                    share(t, far, (x + far) % 4, x).start()

            return 0

        lax.fori_loop(0, ROWS // step, rows, 0)
        for dx in (2, 1, 3):
            cp = share(t, dx, (x + dx) % 4, x)
            if d != 4:
                cp.start()
            started.append(cp)

    def share(t, dx, chunk, slot):
        return pltpu.make_async_remote_copy(
            src_ref=cb.at[t, pl.ds(pl.multiple_of(chunk * CHUNK, CHUNK), CHUNK), :],
            dst_ref=rb.at[t, slot], send_sem=s_x.at[t, dx], recv_sem=r_x.at[t, slot],
            device_id=device(dx=dx), device_id_type=MESH,
        )

    def over_y(i):
        return pltpu.make_async_remote_copy(
            src_ref=red.at[i], dst_ref=yr.at[i], send_sem=s_h.at[i], recv_sem=r_h.at[i],
            device_id=device(dyh=1), device_id_type=MESH,
        )

    def add_x(line, d):
        i = DIST.index(d)
        t = i * 2 + line
        total = cb[t, pl.ds(pl.multiple_of(x * CHUNK, CHUNK), CHUNK), :].astype(jnp.float32)
        for dx in (1, 3, 2):
            src = (x + dx) % 4
            share(t, dx, x, src).wait_recv()
            total += rb[t, src].astype(jnp.float32)
        stays = (y + line) % 2 == yh

        @pl.when(stays)
        def _():
            keep[i] = total

        @pl.when(jnp.logical_not(stays))
        def _():
            red[i] = total.astype(jnp.bfloat16)
            over_y(i).start()

    def final(i, half, to):
        return pltpu.make_async_remote_copy(
            src_ref=done.at[i], dst_ref=fin.at[x, half], send_sem=s_f.at[i], recv_sem=r_f.at[x],
            device_id=(yh * 4 + to, col), device_id_type=MESH,
        )

    def add_y(d):
        i = DIST.index(d)
        over_y(i).wait_recv()
        total = (keep[i] + yr[i].astype(jnp.float32)).astype(jnp.bfloat16)
        at = (z + d + 8) % 8
        half, to = at % 2, at // 2

        @pl.when(to == x)
        def _():
            fin[x, half] = total

        @pl.when(to != x)
        def _():
            done[i] = total
            final(i, half, to).start()

    for part in (H0, H1):
        send("zp", 0, 0, part)
        send("zm", 0, 0, part)
    for part in (H1, H0):
        send("y", 0, 0, part)
    for part in (H0, H1):
        send("c", 0, 0, part)

    load_a.wait()
    for i in range(ROWS // BLOCK):
        for k in range(DEPTH // BLOCK):
            same = sec_ref[col * (ROWS // BLOCK) + i] == sec_ref[row * (DEPTH // BLOCK) + k]
            at = (pl.ds(i * BLOCK, BLOCK), pl.ds(k * BLOCK, BLOCK))
            a[at] = jnp.where(same, a[at], jnp.zeros((BLOCK, BLOCK), a.dtype))

    steps = {"mm": multiply, "ra": add_x, "rb": add_y}
    for name, *args in ORDER:
        if name in steps:
            steps[name](*args)
        else:
            recv(name, *args)
            line, d, _ = args
            for to, part in onward(name, *args):
                send(to, line, d, part)

    for dx in (1, 2, 3):
        src = (x + dx) % 4
        pltpu.make_async_remote_copy(
            src_ref=fin.at[x], dst_ref=fin.at[src], send_sem=s_f.at[0], recv_sem=r_f.at[src],
            device_id=device(dx=dx), device_id_type=MESH,
        ).wait_recv()
    for part in range(4):
        for half in (0, 1):
            at = (pl.ds(part * CHUNK, CHUNK), pl.ds(half * PAIR, PAIR))
            out_ref[at] = fin[part, half]

    for cp in started:
        cp.wait_send()
    for i, d in enumerate(DIST):
        over_y(i).wait_send()
        at = (z + d + 8) % 8

        @pl.when(at // 2 != x)
        def _():
            final(i, at % 2, at // 2).wait_send()


def body(sectors, environment, wavefunction):
    dma = pltpu.SemaphoreType.DMA
    pairs = []
    for link in ("zp", "zm", "y", "c"):
        pairs += [dma((len(LINKS[link]),)), dma((len(LINKS[link]),))]
    return pl.pallas_call(
        kernel,
        out_shape=pltpu.VMEM((ROWS, TILE), jnp.bfloat16),
        in_specs=[
            pl.BlockSpec(memory_space=pltpu.SMEM),
            pl.BlockSpec(memory_space=pl.ANY),
            pl.BlockSpec(memory_space=pl.ANY),
        ],
        out_specs=pl.BlockSpec(memory_space=pltpu.VMEM),
        scratch_shapes=[
            pltpu.VMEM((ROWS, DEPTH), jnp.bfloat16),
            pltpu.VMEM((32 * ITEM, DEPTH), jnp.bfloat16),
            pltpu.VMEM((16, ROWS, PAIR), jnp.bfloat16),
            pltpu.VMEM((16, 4, CHUNK, PAIR), jnp.bfloat16),
            pltpu.VMEM((8, CHUNK, PAIR), jnp.float32),
            pltpu.VMEM((8, CHUNK, PAIR), jnp.bfloat16),
            pltpu.VMEM((8, CHUNK, PAIR), jnp.bfloat16),
            pltpu.VMEM((8, CHUNK, PAIR), jnp.bfloat16),
            pltpu.VMEM((4, 2, CHUNK, PAIR), jnp.bfloat16),
            *pairs,
            dma((16, 4)), dma((16, 4)), dma((8,)), dma((8,)), dma((8,)), dma((4,)), dma((2,)),
        ],
        compiler_params=pltpu.CompilerParams(
            collective_id=0, has_side_effects=True, vmem_limit_bytes=56 << 20
        ),
    )(sectors, environment, wavefunction.T)


def solution(mesh):
    placed = (P(), P("col", "row"), P("row", "col"))
    return jax.shard_map(
        body, mesh=mesh, in_specs=placed, out_specs=P("col", "row"), check_vma=False
    )
```

```python
import jax
import jax.numpy as jnp
from jax import lax
from jax.experimental import pallas as pl
from jax.experimental.pallas import tpu as pltpu
from jax.sharding import PartitionSpec as P

MESH = pl.DeviceIdType.MESH
BLOCK = 256
ITEM = 64
PAIR = 2 * ITEM
ROWS = 768
DEPTH = 3072
HALF = 1664
TILE = 256
CHUNK = ROWS // 4
STEP = 256

H0 = (0, ITEM, 0, HALF)
H1 = (0, ITEM, HALF, DEPTH - HALF)
LO = (0, ITEM // 2, HALF, DEPTH - HALF)
HI = (ITEM // 2, ITEM // 2, HALF, DEPTH - HALF)

DIST = [0, -1, 1, -2, 2, -3, 3, 4]

ZP = [(0, -d, h) for d in range(3) for h in (H0, H1)] + [(1, -d, H1) for d in range(3)] + [(0, -3, H0), (1, -3, LO)]
ZM = [(0, d, h) for d in range(3) for h in (H0, H1)] + [(1, d, H1) for d in range(3)] + [(0, 3, H1), (1, 3, HI)]
YY = [(0, 0, H1)] + [(0, d, H0) for d in DIST]
CC = [(line, d, h) for line in (0, 1) for d in DIST for h in (H0, H1) if (line, d, h) != (1, 4, H1)]
CC += [(1, 4, LO), (1, 4, HI)]
LINKS = {"zp": ZP, "zm": ZM, "y": YY, "c": CC}

ORDER = [
    ("mm", 0, 0),
    ("y", 1, 0, H1),
    ("zp", 0, -1, H0),
    ("zm", 0, 1, H0),
    ("ra", 0, 0),
    ("zp", 0, -1, H1),
    ("zm", 0, 1, H1),
    ("y", 1, 0, H0),
    ("mm", 0, -1),
    ("zp", 1, -1, H1),
    ("zm", 1, 1, H1),
    ("mm", 0, 1),
    ("y", 1, -1, H0),
    ("mm", 1, 0),
    ("mm", 1, -1),
    ("y", 1, 1, H0),
    ("zp", 0, -2, H0),
    ("zm", 0, 2, H0),
    ("ra", 0, -1),
    ("mm", 1, 1),
    ("ra", 1, 0),
    ("zp", 0, -2, H1),
    ("zm", 0, 2, H1),
    ("ra", 0, 1),
    ("mm", 0, -2),
    ("y", 1, -2, H0),
    ("zm", 1, 2, H1),
    ("mm", 0, 2),
    ("ra", 1, -1),
    ("ra", 1, 1),
    ("y", 1, 2, H0),
    ("zm", 0, 3, H0),
    ("zp", 0, -3, H0),
    ("zp", 1, -2, H1),
    ("mm", 1, 2),
    ("zp", 0, -3, H1),
    ("zm", 0, 3, H1),
    ("mm", 1, -2),
    ("mm", 0, -3),
    ("y", 1, 3, H0),
    ("zm", 1, 3, H1),
    ("mm", 0, 3),
    ("zp", 0, 4, H0),
    ("mm", 1, 3),
    ("zm", 0, 4, H1),
    ("y", 1, -3, H0),
    ("zp", 1, -3, H1),
    ("mm", 0, 4),
    ("zm", 1, 4, HI),
    ("mm", 1, -3),
    ("y", 1, 4, H0),
    ("zp", 1, 4, LO),
    ("ra", 0, -2),
    ("ra", 0, 2),
    ("ra", 1, 2),
    ("ra", 1, -2),
    ("ra", 0, -3),
    ("mm", 1, 4),
    ("ra", 0, 3),
    ("ra", 0, 4),
    ("rb", 0),
    ("rb", -1),
    ("rb", 1),
    ("rb", -2),
    ("ra", 1, -3),
    ("ra", 1, 3),
    ("ra", 1, 4),
    ("rb", -3),
    ("rb", 3),
    ("rb", 2),
    ("rb", 4),
]


def onward(link, line, d, part):
    to = [("c", part)]
    if link == "y":
        return to + ([("zp", part), ("zm", part)] if part == H1 else [])
    if line == 0 and part == H0:
        to.append(("y", part))
    if abs(d) < 3:
        to.insert(0, (link, part))
    elif abs(d) == 3 and line == 1:
        to.insert(0, (link, LO if link == "zp" else HI))
    elif abs(d) == 3 and part == (H0 if link == "zp" else H1):
        to.insert(0, (link, part))
    return to


def kernel(sec_ref, env_ref, wave_ref, out_ref, a, g, cb, rb, keep, red, yr, done, fin,
           s_zp, r_zp, s_zm, r_zm, s_y, r_y, s_c, r_c, s_x, r_x, s_h, r_h, s_f, r_f, local):
    row, col = lax.axis_index("row"), lax.axis_index("col")
    yh, x = row // 4, row % 4
    y, z, c = col // 16, (col // 2) % 8, col % 2

    def device(dyh=0, dx=0, dy=0, dz=0, dc=0):
        return (
            (yh + dyh) % 2 * 4 + (x + dx) % 4,
            (y + dy) % 2 * 16 + (z + dz + 8) % 8 * 2 + (c + dc) % 2,
        )

    load_a = pltpu.make_async_copy(env_ref, a, local.at[0])
    own = pl.ds(pl.multiple_of(col * ITEM, ITEM), ITEM)
    load_b = pltpu.make_async_copy(wave_ref, g.at[own, :], local.at[1])
    load_b.start()
    load_a.start()

    barrier = pltpu.get_barrier_semaphore()
    greet = [device(dz=1), device(dz=-1), device(dy=1), device(dc=1), device(dyh=1)]
    greet += [device(dx=d) for d in (1, 2, 3)]
    for peer in greet:
        pl.semaphore_signal(barrier, inc=1, device_id=peer, device_id_type=MESH)
    load_b.wait()
    pl.semaphore_wait(barrier, len(greet))

    sems = {"zp": (s_zp, r_zp), "zm": (s_zm, r_zm), "y": (s_y, r_y), "c": (s_c, r_c)}
    peers = {"zp": device(dz=1), "zm": device(dz=-1), "y": device(dy=1), "c": device(dc=1)}
    moves = {"zp": (0, -1, 0), "zm": (0, 1, 0), "y": (1, 0, 0), "c": (0, 0, 1)}
    started = []

    def piece(line, d, part, parity):
        r0, nr, k0, nk = part
        j = (y + line) % 2 * 16 + (z + d + 8) % 8 * 2 + (c + parity) % 2
        return g.at[pl.ds(pl.multiple_of(j * ITEM + r0, 32), nr), pl.ds(k0, nk)]

    def copy(link, ref, i):
        return pltpu.make_async_remote_copy(
            src_ref=ref, dst_ref=ref, send_sem=sems[link][0].at[i], recv_sem=sems[link][1].at[i],
            device_id=peers[link], device_id_type=MESH,
        )

    def send(link, line, d, part):
        cp = copy(link, piece(line, d, part, 0), LINKS[link].index((line, d, part)))
        cp.start()
        started.append(cp)

    def recv(link, line, d, part):
        dl, dz, dc = moves[link]
        sd = d - dz
        sd = {-4: 4, 5: -3, -5: 3}.get(sd, sd)
        i = LINKS[link].index(((line + dl) % 2, sd, part))
        copy(link, piece(line, d, part, dc), i).wait_recv()

    def multiply(line, d):
        for part in (H0, LO, HI) if (line, d) == (1, 4) else (H0, H1):
            recv("c", line, d, part)
        t = DIST.index(d) * 2 + line
        base = (y + line) % 2 * (16 * ITEM) + (z + d + 8) % 8 * PAIR
        block = pl.ds(pl.multiple_of(base, PAIR), PAIR)

        step = CHUNK if d == 4 else STEP

        def rows(m, _):
            far = 2 - m + m // 2 * (3 - 2 * (m % 2))
            at = (x + far) % 4 if d == 4 else m
            at = pl.ds(pl.multiple_of(at * step, step), step)
            cb[t, at, :] = lax.dot_general(
                a[at, :], g[block, :], (((1,), (1,)), ((), ())), preferred_element_type=jnp.float32
            ).astype(jnp.bfloat16)
            if d == 4:

                @pl.when(far != 0)
                def _():
                    share(t, far, (x + far) % 4, x).start()

            return 0

        lax.fori_loop(0, ROWS // step, rows, 0)
        for dx in (2, 1, 3):
            cp = share(t, dx, (x + dx) % 4, x)
            if d != 4:
                cp.start()
            started.append(cp)

    def share(t, dx, chunk, slot):
        return pltpu.make_async_remote_copy(
            src_ref=cb.at[t, pl.ds(pl.multiple_of(chunk * CHUNK, CHUNK), CHUNK), :],
            dst_ref=rb.at[t, slot], send_sem=s_x.at[t, dx], recv_sem=r_x.at[t, slot],
            device_id=device(dx=dx), device_id_type=MESH,
        )

    def over_y(i):
        return pltpu.make_async_remote_copy(
            src_ref=red.at[i], dst_ref=yr.at[i], send_sem=s_h.at[i], recv_sem=r_h.at[i],
            device_id=device(dyh=1), device_id_type=MESH,
        )

    def add_x(line, d):
        i = DIST.index(d)
        t = i * 2 + line
        total = cb[t, pl.ds(pl.multiple_of(x * CHUNK, CHUNK), CHUNK), :].astype(jnp.float32)
        for dx in (1, 3, 2):
            src = (x + dx) % 4
            share(t, dx, x, src).wait_recv()
            total += rb[t, src].astype(jnp.float32)
        stays = (y + line) % 2 == yh

        @pl.when(stays)
        def _():
            keep[i] = total

        @pl.when(jnp.logical_not(stays))
        def _():
            red[i] = total.astype(jnp.bfloat16)
            over_y(i).start()

    def final(i, half, to):
        return pltpu.make_async_remote_copy(
            src_ref=done.at[i], dst_ref=fin.at[x, half], send_sem=s_f.at[i], recv_sem=r_f.at[x],
            device_id=(yh * 4 + to, col), device_id_type=MESH,
        )

    def add_y(d):
        i = DIST.index(d)
        over_y(i).wait_recv()
        total = (keep[i] + yr[i].astype(jnp.float32)).astype(jnp.bfloat16)
        at = (z + d + 8) % 8
        half, to = at % 2, at // 2

        @pl.when(to == x)
        def _():
            fin[x, half] = total

        @pl.when(to != x)
        def _():
            done[i] = total
            final(i, half, to).start()

    for part in (H0, H1):
        send("zp", 0, 0, part)
        send("zm", 0, 0, part)
    for part in (H1, H0):
        send("y", 0, 0, part)
    for part in (H0, H1):
        send("c", 0, 0, part)

    load_a.wait()
    for i in range(ROWS // BLOCK):
        for k in range(DEPTH // BLOCK):
            same = sec_ref[col * (ROWS // BLOCK) + i] == sec_ref[row * (DEPTH // BLOCK) + k]
            at = (pl.ds(i * BLOCK, BLOCK), pl.ds(k * BLOCK, BLOCK))
            a[at] = jnp.where(same, a[at], jnp.zeros((BLOCK, BLOCK), a.dtype))

    steps = {"mm": multiply, "ra": add_x, "rb": add_y}
    for name, *args in ORDER:
        if name in steps:
            steps[name](*args)
        else:
            recv(name, *args)
            line, d, _ = args
            for to, part in onward(name, *args):
                send(to, line, d, part)

    for dx in (1, 2, 3):
        src = (x + dx) % 4
        pltpu.make_async_remote_copy(
            src_ref=fin.at[x], dst_ref=fin.at[src], send_sem=s_f.at[0], recv_sem=r_f.at[src],
            device_id=device(dx=dx), device_id_type=MESH,
        ).wait_recv()
    for part in range(4):
        for half in (0, 1):
            at = (pl.ds(part * CHUNK, CHUNK), pl.ds(half * PAIR, PAIR))
            out_ref[at] = fin[part, half]

    for cp in started:
        cp.wait_send()
    for i, d in enumerate(DIST):
        over_y(i).wait_send()
        at = (z + d + 8) % 8

        @pl.when(at // 2 != x)
        def _():
            final(i, at % 2, at // 2).wait_send()


def body(sectors, environment, wavefunction):
    dma = pltpu.SemaphoreType.DMA
    pairs = []
    for link in ("zp", "zm", "y", "c"):
        pairs += [dma((len(LINKS[link]),)), dma((len(LINKS[link]),))]
    return pl.pallas_call(
        kernel,
        out_shape=pltpu.VMEM((ROWS, TILE), jnp.bfloat16),
        in_specs=[
            pl.BlockSpec(memory_space=pltpu.SMEM),
            pl.BlockSpec(memory_space=pl.ANY),
            pl.BlockSpec(memory_space=pl.ANY),
        ],
        out_specs=pl.BlockSpec(memory_space=pltpu.VMEM),
        scratch_shapes=[
            pltpu.VMEM((ROWS, DEPTH), jnp.bfloat16),
            pltpu.VMEM((32 * ITEM, DEPTH), jnp.bfloat16),
            pltpu.VMEM((16, ROWS, PAIR), jnp.bfloat16),
            pltpu.VMEM((16, 4, CHUNK, PAIR), jnp.bfloat16),
            pltpu.VMEM((8, CHUNK, PAIR), jnp.float32),
            pltpu.VMEM((8, CHUNK, PAIR), jnp.bfloat16),
            pltpu.VMEM((8, CHUNK, PAIR), jnp.bfloat16),
            pltpu.VMEM((8, CHUNK, PAIR), jnp.bfloat16),
            pltpu.VMEM((4, 2, CHUNK, PAIR), jnp.bfloat16),
            *pairs,
            dma((16, 4)), dma((16, 4)), dma((8,)), dma((8,)), dma((8,)), dma((4,)), dma((2,)),
        ],
        compiler_params=pltpu.CompilerParams(
            collective_id=0, has_side_effects=True, vmem_limit_bytes=56 << 20
        ),
    )(sectors, environment, wavefunction.T)


def solution(mesh):
    placed = (P(), P("col", "row"), P("row", "col"))
    return jax.shard_map(
        body, mesh=mesh, in_specs=placed, out_specs=P("col", "row"), check_vma=False
    )
```
